32 devices in a mesh: head: 4 (over y, x), ctx: 8 (over z, core).
Axes of the slice: x: 2, y: 2, z: 4, core: 2. Of those that a mesh axis runs over, the one named last changes fastest.
Arguments:
- query_rows: bfloat16 [4096, 2048], P(('ctx', 'head')), may hold values from -6 to 6
- key_rows: bfloat16 [4096, 2048], P(('ctx', 'head')), may hold values from -6 to 6
- value_rows: bfloat16 [4096, 4096], P(('ctx', 'head')), may hold values from -6 to 6
- gate_rows: bfloat16 [4096, 4096], P(('ctx', 'head')), may hold values from -6 to 6
- write_strength: bfloat16 [4096, 32], P(('ctx', 'head')), may hold values from 0 to 1
- log_decay: bfloat16 [4096, 32], P(('ctx', 'head')), may hold values from -1 to 0
- norm_gain: float32 [128], replicated, may hold values from 0.1 to 1.9
Outputs:
- mixed_out: bfloat16 [4096, 4096], P(('ctx', 'head'))
The draws below stay inside these ranges and needn't reach their ends.
All inputs are finite; a program needn't handle non-finite values.
Results may differ from the reference program's by a relative error of at most 0.0049.
Values may be sent and summed in bfloat16 or wider, within the bound.
A program may use at most 192 MiB of HBM per device.

```python
import math
import jax
import jax.numpy as jnp
from jax import lax

HK = 16
VALUE_HEADS = 32
DK = 128
DV = 128
C = 64
SEQUENCE_TOKENS = 4096


def head_kinds(key):
    picker = jax.random.fold_in(key, 11)
    fast = jax.random.randint(picker, (VALUE_HEADS,), 0, 2) == 1
    return fast


def draw_write_strength(key, part):
    fast = head_kinds(key)
    first, second, third = jax.random.split(jax.random.fold_in(key, 21), 3)
    fast_beta = jax.random.uniform(first, (SEQUENCE_TOKENS, VALUE_HEADS), jnp.float32, 0.2, 1.0)
    slow_level = jnp.exp(jax.random.uniform(second, (VALUE_HEADS,), jnp.float32, math.log(0.3), 0.0)) * DK / SEQUENCE_TOKENS
    slow_beta = slow_level[None, :] * jax.random.uniform(third, (SEQUENCE_TOKENS, VALUE_HEADS), jnp.float32, 0.5, 2.0)
    return jnp.where(fast[None, :], fast_beta, slow_beta).astype(jnp.bfloat16)


def draw_log_decay(key, part):
    fast = head_kinds(key)
    first, second, third, fourth_factor, fifth_factor = jax.random.split(jax.random.fold_in(key, 31), 5)
    fast_rate = jnp.exp(jax.random.uniform(first, (VALUE_HEADS,), jnp.float32, math.log(1.0 / 50.0), math.log(1.0 / 30.0)))
    slow_rate = jnp.exp(jax.random.uniform(second, (VALUE_HEADS,), jnp.float32, math.log(0.1), math.log(0.4))) / SEQUENCE_TOKENS
    decay_speed = jnp.where(fast, fast_rate, slow_rate)
    coarse_estimate = jax.random.uniform(third, (SEQUENCE_TOKENS, VALUE_HEADS), jnp.float32, 0.5, 2.0)
    token_group = jax.random.randint(fourth_factor, (SEQUENCE_TOKENS, VALUE_HEADS), 0, SEQUENCE_TOKENS // 2) == 0
    token_group_length = jax.random.uniform(fifth_factor, (SEQUENCE_TOKENS, VALUE_HEADS), jnp.float32, 0.22, 0.69)
    return (-(decay_speed[None, :] * coarse_estimate + jnp.where(token_group, token_group_length, 0.0))).astype(jnp.bfloat16)


def levels(own_key, extent, cuts, least, top_value):
    def one(axis_at, shards_of):
        heights = jax.random.uniform(jax.random.fold_in(jax.random.fold_in(own_key, 6), axis_at), (shards_of,), jnp.float32, least / len(cuts), top_value / len(cuts))
        return jnp.repeat(jnp.exp(heights), extent[axis_at] // shards_of).reshape((-1,) + (1,) * (len(extent) - axis_at - 1))

    factor_of = one(*cuts[0])
    for cut in cuts[1:]:
        factor_of = factor_of * one(*cut)
    return factor_of


def gaussian(key, shape, deviation, bound, shards=(), held_as=jnp.bfloat16):
    values = deviation * jax.random.normal(key, shape, jnp.float32)
    if shards:
        values = values * levels(key, shape, shards, -0.22, 0.18)
    return jnp.clip(values, -bound, bound).astype(held_as)


def setup_inputs(seed: int = 0) -> dict:
    keys = jax.random.split(jax.random.key(seed), 8)
    query_rows = gaussian(keys[0], (SEQUENCE_TOKENS, HK * DK), 1.0, 6.0, ((0, 32),))
    key_rows = gaussian(keys[1], (SEQUENCE_TOKENS, HK * DK), 1.0, 6.0, ((0, 32),))
    value_rows = gaussian(keys[2], (SEQUENCE_TOKENS, VALUE_HEADS * DV), 1.0, 6.0, ((0, 32),))
    gate_rows = gaussian(keys[3], (SEQUENCE_TOKENS, VALUE_HEADS * DV), 1.0, 6.0, ((0, 32),))
    write_strength = draw_write_strength(jax.random.fold_in(keys[7], 71), 0)
    log_decay = draw_log_decay(jax.random.fold_in(keys[7], 71), 0)
    norm_gain = jnp.clip(1.0 + 0.18 * jax.random.normal(keys[6], (DV,), jnp.float32), 0.1, 1.9)
    return {"query_rows": query_rows, "key_rows": key_rows, "value_rows": value_rows, "gate_rows": gate_rows, "write_strength": write_strength, "log_decay": log_decay, "norm_gain": norm_gain}


def unit_rows(vectors):
    return vectors * lax.rsqrt(lax.optimization_barrier(jnp.sum(vectors * vectors, axis=-1, keepdims=True)) + 1e-06)

def unit_lower_apply(system_off, right_hand):
    highest = lax.Precision.HIGHEST
    group_len = system_off.shape[-1]
    rounds = (group_len - 1).bit_length()
    power = -system_off
    solved = right_hand
    for index in range(rounds):
        solved = solved + jnp.einsum('...ij,...jk->...ik', power, solved, precision=highest)
        if index + 1 < rounds:
            power = jnp.einsum('...ij,...jk->...ik', power, power, precision=highest)
    return solved

def group_terms(query_blk, key_blk, value_blk, beta_blk, decay_blk):
    highest = lax.Precision.HIGHEST
    group_len = query_blk.shape[-2]
    cumulative = jnp.cumsum(decay_blk, axis=-1)
    gaps_log = cumulative[..., :, None] - cumulative[..., None, :]
    position = jnp.arange(group_len)
    causal = position[:, None] >= position[None, :]
    strict = position[:, None] > position[None, :]
    weights = jnp.where(causal, jnp.exp(jnp.minimum(gaps_log, 0.0)), 0.0)
    key_inner = jnp.einsum('...id,...jd->...ij', key_blk, key_blk, precision=highest)
    system_off = jnp.where(strict, beta_blk[..., :, None] * weights * key_inner, 0.0)
    growth = jnp.exp(cumulative)
    right_hand = jnp.concatenate([beta_blk[..., None] * value_blk, (beta_blk * growth)[..., None] * key_blk], axis=-1)
    solved = unit_lower_apply(system_off, right_hand)
    value_width = value_blk.shape[-1]
    fresh_vals = solved[..., :value_width]
    key_factor = solved[..., value_width:]
    to_end = jnp.exp(cumulative[..., -1:] - cumulative)
    key_scaled = to_end[..., None] * key_blk
    identity = jnp.eye(key_blk.shape[-1], dtype=jnp.float32)
    transition = growth[..., -1, None, None] * identity - jnp.einsum('...cd,...ce->...de', key_scaled, key_factor, precision=highest)
    written = jnp.einsum('...cd,...ce->...de', key_scaled, fresh_vals, precision=highest)
    scores = jnp.einsum('...id,...jd->...ij', query_blk, key_blk, precision=highest) * weights
    local_out = jnp.einsum('...ij,...je->...ie', scores, fresh_vals, precision=highest)
    reader = growth[..., None] * query_blk - jnp.einsum('...ij,...jd->...id', scores, key_factor, precision=highest)
    return (transition, written, reader, local_out)

def gated_norm(core, gate_rows, norm_gain):
    values = lax.optimization_barrier(core).astype(jnp.float32)
    values = values.reshape(core.shape[0], -1, norm_gain.shape[0])
    scaled = values * lax.rsqrt(lax.optimization_barrier(jnp.mean(values * values, axis=-1, keepdims=True)) + 1e-06)
    gates = gate_rows.astype(jnp.float32).reshape(values.shape)
    result = scaled * norm_gain * jax.nn.silu(gates)
    return result.reshape(core.shape[0], -1).astype(jnp.bfloat16)

def reference(query_rows, key_rows, value_rows, gate_rows, write_strength, log_decay, norm_gain):
    highest = lax.Precision.HIGHEST
    seq_len = query_rows.shape[0]
    queries = jnp.repeat(unit_rows(query_rows.astype(jnp.float32).reshape(seq_len, HK, DK)), VALUE_HEADS // HK, axis=1)
    keys_all = jnp.repeat(unit_rows(key_rows.astype(jnp.float32).reshape(seq_len, HK, DK)), VALUE_HEADS // HK, axis=1)
    values = value_rows.astype(jnp.float32).reshape(seq_len, VALUE_HEADS, DV)
    strength = write_strength.astype(jnp.float32)
    decay_log = log_decay.astype(jnp.float32)
    blocks = seq_len // C

    def blocked(array):
        return jnp.swapaxes(array.reshape((blocks, C) + array.shape[1:]), 1, 2)

    def advance(state, inputs):
        transition, written, reader, local_out = group_terms(*inputs)
        output = local_out + jnp.einsum('hcd,hde->hce', reader, state, precision=highest)
        state = jnp.einsum('hde,hef->hdf', transition, state, precision=highest) + written
        return (state, output)
    start_state = jnp.zeros((VALUE_HEADS, DK, DV), jnp.float32)
    final_state, outputs = lax.scan(advance, start_state, (blocked(queries), blocked(keys_all), blocked(values), blocked(strength), blocked(decay_log)))
    core = jnp.swapaxes(outputs, 1, 2).reshape(seq_len, VALUE_HEADS * DV).astype(jnp.bfloat16)
    return gated_norm(core, gate_rows, norm_gain)
```

```python
import functools

import jax
import jax.numpy as jnp
from jax import lax
from jax.experimental import pallas as pl
from jax.experimental.pallas import tpu as pltpu
from jax.sharding import PartitionSpec as P

D = 128
B = 128
F32 = jnp.float32
BF = jnp.bfloat16
MESH = pl.DeviceIdType.MESH


def split(x):
    hi = x.astype(BF)
    return hi, (x - hi.astype(F32)).astype(BF)


def dot(a, b):
    return jnp.dot(a, b, preferred_element_type=F32)


def dot_t(a, b):
    return lax.dot_general(a, b, (((1,), (1,)), ((), ())), preferred_element_type=F32)


def dot_b(a, b):
    return dot(a.astype(BF), b.astype(BF))


def dot_fe(a, b):
    hi, lo = split(a)
    return dot(jnp.concatenate([hi, lo], 1), jnp.concatenate([b, b], 0))


def dot_ef(a, b):
    hi, lo = split(b)
    return dot(jnp.concatenate([a, a], 1), jnp.concatenate([hi, lo], 0))


def dot_ff(a, b):
    ah, al = split(a)
    bh, bl = split(b)
    return dot(jnp.concatenate([ah, ah], 1), jnp.concatenate([bh, bl], 0)) + dot(al, bh)


def exchange_kernel(n, q, k, v, be, de, qo, ko, vo, beo, deo, ssem, rsem, lsem):
    me = lax.axis_index("head")
    barrier = pltpu.get_barrier_semaphore()
    for s in range(1, n):
        pl.semaphore_signal(barrier, inc=1, device_id={"head": lax.rem(me + s, n)}, device_id_type=MESH)
    pl.semaphore_wait(barrier, n - 1)
    t = q.shape[0]
    rows = pl.ds(pl.multiple_of(me * t, t), t)
    arrays = [(de, deo, None), (be, beo, None), (k, ko, k.shape[1] // n), (v, vo, v.shape[1] // n), (q, qo, q.shape[1] // n)]

    def piece(src, dest, w):
        if w is None:
            return src
        return src.at[:, pl.ds(pl.multiple_of(dest * w, w), w)]

    copies = []
    for i, (src, dst, w) in enumerate(arrays):
        for s in range(1, n):
            dest = lax.rem(me + s, n)
            copies.append(
                pltpu.make_async_remote_copy(
                    src_ref=piece(src, dest, w),
                    dst_ref=dst.at[rows, :],
                    send_sem=ssem.at[i, s],
                    recv_sem=rsem.at[i, s],
                    device_id={"head": dest},
                    device_id_type=MESH,
                )
            )
            copies[-1].start()
    local = []
    for i, (src, dst, w) in enumerate(arrays):
        local.append(pltpu.make_async_copy(piece(src, me, w), dst.at[rows, :], lsem.at[i]))
        local[-1].start()
    for c in local:
        c.wait()
    for c in copies:
        c.wait()


def exchange(n, q, k, v, be, de):
    t = q.shape[0] * n
    any_spec = pl.BlockSpec(memory_space=pl.ANY)
    return pl.pallas_call(
        functools.partial(exchange_kernel, n),
        out_shape=[
            jax.ShapeDtypeStruct((t, q.shape[1] // n), BF),
            jax.ShapeDtypeStruct((t, k.shape[1] // n), BF),
            jax.ShapeDtypeStruct((t, v.shape[1] // n), BF),
            jax.ShapeDtypeStruct((t, be.shape[1]), BF),
            jax.ShapeDtypeStruct((t, de.shape[1]), BF),
        ],
        in_specs=[any_spec] * 5,
        out_specs=[any_spec] * 5,
        scratch_shapes=[
            pltpu.SemaphoreType.DMA((5, n)),
            pltpu.SemaphoreType.DMA((5, n)),
            pltpu.SemaphoreType.DMA((5,)),
        ],
        compiler_params=pltpu.CompilerParams(collective_id=0, has_side_effects=True),
    )(q, k, v, be, de)


def unit_lower_inverse(lows, ii, jj):
    eye = (ii == jj).astype(F32)

    def same(w):
        return (ii // w) == (jj // w)

    base = same(16)
    p = [jnp.where(base, -x, 0.0) for x in lows]
    t = [eye + x for x in p]
    for _ in range(3):
        pb = [x.astype(BF) for x in p]
        p = [dot(x, x) for x in pb]
        t = [y + dot_b(y, x) for y, x in zip(t, p)]
    w = 16
    while w < B:
        off = same(2 * w) & ~same(w)
        tb = [y.astype(BF) for y in t]
        z = [dot(jnp.where(off, x, 0.0).astype(BF), y) for x, y in zip(lows, tb)]
        t = [y - dot(yb, x.astype(BF)) for y, yb, x in zip(t, tb, z)]
        w *= 2
    return t


def block_kernel(heads, q_ref, k_ref, v_ref, be_ref, de_ref, base_ref, r_ref, x_ref):
    me = lax.axis_index("head")
    blocks = q_ref.shape[0] // B
    kheads = q_ref.shape[1] // D
    per = heads // kheads
    wide = be_ref.shape[1]
    ii = lax.broadcasted_iota(jnp.int32, (B, B), 0)
    jj = lax.broadcasted_iota(jnp.int32, (B, B), 1)
    eye = ii == jj
    causal = ii >= jj
    strict = ii > jj
    low = causal.astype(BF)
    upp = (ii <= jj).astype(BF)
    after = (ii < jj).astype(BF)
    ones = jnp.ones((B, B), BF)
    sel = (
        lax.broadcasted_iota(jnp.int32, (wide, heads), 0)
        == lax.broadcasted_iota(jnp.int32, (wide, heads), 1) + me * heads
    ).astype(BF)
    sel_t = (
        lax.broadcasted_iota(jnp.int32, (heads, wide), 1)
        == lax.broadcasted_iota(jnp.int32, (heads, wide), 0) + me * heads
    ).astype(BF)
    start = jnp.concatenate([jnp.zeros((B, D), F32), eye.astype(F32)], 1)
    for h in range(heads):
        x_ref[h] = start

    def one(b, carry):
        rows = pl.ds(pl.multiple_of(b * B, B), B)
        de = de_ref[rows, :]
        be = be_ref[rows, :]
        dcol = dot(de, sel).astype(BF)
        drow = dot_t(sel_t, de).astype(BF)
        bcol = dot(low, dcol)
        brow = dot(drow, upp)
        becol = dot(be, sel)
        berow = dot_t(sel_t, be)
        gcol = jnp.exp(bcol)
        grow = jnp.exp(brow)
        ecol = jnp.exp(dot(after, dcol))
        lastcol = jnp.exp(dot(ones, dcol))
        ks, qs, rkc, rkr, rqc, gn, hn = [], [], [], [], [], [], []
        for a in range(kheads):
            k = k_ref[rows, a * D : (a + 1) * D]
            q = q_ref[rows, a * D : (a + 1) * D]
            g = dot_t(k, k)
            diag = jnp.where(eye, g, 0.0)
            rc = lax.rsqrt(jnp.sum(diag, axis=1, keepdims=True) + 1e-6)
            rr = lax.rsqrt(jnp.sum(diag, axis=0, keepdims=True) + 1e-6)
            qf = q.astype(F32)
            qc = lax.rsqrt(jnp.sum(qf * qf, axis=1, keepdims=True) + 1e-6)
            ks.append(k)
            qs.append(q)
            rkc.append(rc)
            rkr.append(rr)
            rqc.append(qc)
            gn.append(g * rc * rr)
            hn.append(dot_t(q, k) * qc * rr)
        lows, reads = [], []
        for h in range(heads):
            a = h // per
            gap = bcol[:, h : h + 1] - brow[h : h + 1, :]
            wts = jnp.where(causal, jnp.exp(jnp.minimum(gap, 0.0)), 0.0)
            lows.append(jnp.where(strict, becol[:, h : h + 1] * wts * gn[a], 0.0))
            reads.append((wts * hn[a]).astype(BF))
        inv = unit_lower_inverse(lows, ii, jj)
        xs = [x_ref[h] for h in range(heads)]
        fresh, ds = [], []
        for h in range(heads):
            a = h // per
            br = berow[h : h + 1, :]
            u = dot_fe(inv[h] * br, v_ref[rows, h * D : (h + 1) * D])
            w = dot_fe(inv[h] * (br * grow[h : h + 1, :] * rkr[a]), ks[a])
            fresh.append(u)
            ds.append(w)
        for h in range(heads):
            ds[h] = jnp.concatenate([fresh[h], jnp.zeros((B, D), F32)], 1) - dot_ff(ds[h], xs[h])
        kts = [jnp.transpose(k) for k in ks]
        for h in range(heads):
            a = h // per
            x_ref[h] = lastcol[:, h : h + 1] * xs[h] + dot_ef(kts[a], (ecol[:, h : h + 1] * rkc[a]) * ds[h])
        for h in range(heads):
            a = h // per
            out = dot_ef(reads[h], ds[h]) + (gcol[:, h : h + 1] * rqc[a]) * dot_ef(qs[a], xs[h])
            base_ref[h, rows, :] = out[:, :D]
            r_ref[h, rows, :] = out[:, D:]
        return carry

    lax.fori_loop(0, blocks, one, 0)


def block_factors(heads, q, k, v, be, de):
    t = q.shape[0]
    spec = pl.BlockSpec(memory_space=pltpu.VMEM)
    return pl.pallas_call(
        functools.partial(block_kernel, heads),
        out_shape=[
            jax.ShapeDtypeStruct((heads, t, D), F32),
            jax.ShapeDtypeStruct((heads, t, D), F32),
            jax.ShapeDtypeStruct((heads, D, 2 * D), F32),
        ],
        in_specs=[spec] * 5,
        out_specs=[spec] * 3,
        compiler_params=pltpu.CompilerParams(vmem_limit_bytes=48 << 20),
    )(q, k, v, be, de)


def finish_kernel(n, m, heads, base, r, xf, gate, gain, out, sin, sout, core, got, cs, cr, ss, rs):
    me = lax.axis_index("head")
    c = lax.axis_index("ctx")
    t = gate.shape[0]
    barrier = pltpu.get_barrier_semaphore()
    for s in range(1, n):
        pl.semaphore_signal(barrier, inc=1, device_id={"head": lax.rem(me + s, n)}, device_id_type=MESH)

    for s in (1, m - 1):
        pl.semaphore_signal(barrier, inc=1, device_id={"ctx": lax.rem(c + s, m)}, device_id_type=MESH)
    pl.semaphore_wait(barrier, n + 1)

    def chain(h):
        return pltpu.make_async_remote_copy(
            src_ref=sout.at[h],
            dst_ref=sin.at[h],
            send_sem=cs.at[h],
            recv_sem=cr.at[h],
            device_id={"ctx": lax.rem(c + 1, m)},
            device_id_type=MESH,
        )

    def send(h, s):
        dest = lax.rem(me + s, n)
        return pltpu.make_async_remote_copy(
            src_ref=core.at[h, pl.ds(pl.multiple_of(dest * t, t), t), :],
            dst_ref=got.at[me * heads + h],
            send_sem=ss.at[h, s],
            recv_sem=rs.at[h, s],
            device_id={"head": dest},
            device_id_type=MESH,
        )

    def head_step(h, carry):
        @pl.when(c > 0)
        def _():
            chain(h).wait_recv()

        @pl.when(c == 0)
        def _():
            sin[h] = jnp.zeros((D, D), F32)

        state = sin[h]

        @pl.when(c < m - 1)
        def _():
            sout[h] = dot_ff(xf[h, :, D:], state) + xf[h, :, :D]
            chain(h).start()

        core[h] = (base[h] + dot_ff(r[h], state)).astype(BF)
        for s in range(1, n):
            send(h, s).start()
        got[me * heads + h] = core[h, pl.ds(pl.multiple_of(me * t, t), t), :]
        return carry

    lax.fori_loop(0, heads, head_step, 0)
    scale = gain[...]

    def norm(i):
        x = got[i].astype(F32)
        cols = pl.ds(pl.multiple_of(i * D, D), D)
        g = gate[:, cols].astype(F32)
        y = x * lax.rsqrt(jnp.mean(x * x, axis=-1, keepdims=True) + 1e-6)
        out[:, cols] = (y * scale * (g / (1.0 + jnp.exp(-g)))).astype(BF)

    def own(h, carry):
        norm(me * heads + h)
        return carry

    lax.fori_loop(0, heads, own, 0)

    def others(h, carry):
        for s in range(1, n):
            send(h, s).wait_recv()
            norm(lax.rem(me + n - s, n) * heads + h)
        return carry

    lax.fori_loop(0, heads, others, 0)

    def drain(h, carry):
        for s in range(1, n):
            send(h, s).wait_send()

        @pl.when(c < m - 1)
        def _():
            chain(h).wait_send()

        return carry

    lax.fori_loop(0, heads, drain, 0)


def finish(n, m, heads, base, r, xf, gate, gain):
    t, width = gate.shape
    spec = pl.BlockSpec(memory_space=pltpu.VMEM)
    return pl.pallas_call(
        functools.partial(finish_kernel, n, m, heads),
        out_shape=jax.ShapeDtypeStruct((t, width), BF),
        in_specs=[spec] * 5,
        out_specs=spec,
        scratch_shapes=[
            pltpu.VMEM((heads, D, D), F32),
            pltpu.VMEM((heads, D, D), F32),
            pltpu.VMEM((heads, t * n, D), BF),
            pltpu.VMEM((heads * n, t, D), BF),
            pltpu.SemaphoreType.DMA((heads,)),
            pltpu.SemaphoreType.DMA((heads,)),
            pltpu.SemaphoreType.DMA((heads, n)),
            pltpu.SemaphoreType.DMA((heads, n)),
        ],
        compiler_params=pltpu.CompilerParams(
            collective_id=1, has_side_effects=True, vmem_limit_bytes=48 << 20
        ),
    )(base, r, xf, gate, gain)


def solution(mesh):
    n, m = mesh.shape["head"], mesh.shape["ctx"]

    def local(q, k, v, gate, be, de, gain):
        heads = v.shape[1] // D // n
        q, k, v, be, de = exchange(n, q, k, v, be, de)
        base, r, xf = block_factors(heads, q, k, v, be, de)
        return finish(n, m, heads, base, r, xf, gate, gain.reshape(1, D))

    rows = P(("ctx", "head"), None)
    return jax.shard_map(
        local, mesh=mesh, in_specs=(rows,) * 6 + (P(),), out_specs=rows, check_vma=False
    )
```

```python
import functools

import jax
import jax.numpy as jnp
from jax import lax
from jax.experimental import pallas as pl
from jax.experimental.pallas import tpu as pltpu
from jax.sharding import PartitionSpec as P

D = 128
B = 128
F32 = jnp.float32
BF = jnp.bfloat16
MESH = pl.DeviceIdType.MESH


def split(x):
    hi = x.astype(BF)
    return hi, (x - hi.astype(F32)).astype(BF)


def dot(a, b):
    return jnp.dot(a, b, preferred_element_type=F32)


def dot_t(a, b):
    return lax.dot_general(a, b, (((1,), (1,)), ((), ())), preferred_element_type=F32)


def dot_b(a, b):
    return dot(a.astype(BF), b.astype(BF))


def dot_fe(a, b):
    hi, lo = split(a)
    return dot(jnp.concatenate([hi, lo], 1), jnp.concatenate([b, b], 0))


def dot_ef(a, b):
    hi, lo = split(b)
    return dot(jnp.concatenate([a, a], 1), jnp.concatenate([hi, lo], 0))


def dot_ff(a, b):
    ah, al = split(a)
    bh, bl = split(b)
    return dot(jnp.concatenate([ah, ah], 1), jnp.concatenate([bh, bl], 0)) + dot(al, bh)


def unit_lower_inverse(lows, ii, jj):
    eye = (ii == jj).astype(F32)

    def same(w):
        return (ii // w) == (jj // w)

    base = same(16)
    p = [jnp.where(base, -x, 0.0) for x in lows]
    t = [eye + x for x in p]
    for _ in range(3):
        pb = [x.astype(BF) for x in p]
        p = [dot(x, x) for x in pb]
        t = [y + dot_b(y, x) for y, x in zip(t, p)]
    w = 16
    while w < B:
        off = same(2 * w) & ~same(w)
        tb = [y.astype(BF) for y in t]
        z = [dot(jnp.where(off, x, 0.0).astype(BF), y) for x, y in zip(lows, tb)]
        t = [y - dot(yb, x.astype(BF)) for y, yb, x in zip(t, tb, z)]
        w *= 2
    return t


def fused_kernel(
    n, m, kheads, per,
    q, k, v, be, de, gate_hbm, gain,
    out,
    qb, kb, vb, beb, deb, gate, xf, base, r, sin, sout, core, got,
    es, er, el, fs, fr, fl, gs, cs, cr, ss, rs,
):
    me = lax.axis_index("head")
    c = lax.axis_index("ctx")
    heads = kheads * per
    t = q.shape[0]
    wide = be.shape[0]
    blocks = t * n // B
    barrier = pltpu.get_barrier_semaphore()
    for s in range(1, n):
        pl.semaphore_signal(barrier, inc=1, device_id={"head": lax.rem(me + s, n)}, device_id_type=MESH)
    for s in (1, m - 1):
        pl.semaphore_signal(barrier, inc=1, device_id={"ctx": lax.rem(c + s, m)}, device_id_type=MESH)
    pl.semaphore_wait(barrier, n + 1)

    mine = pl.ds(pl.multiple_of(me * t, t), t)
    small = ((de, deb), (be, beb))
    large = ((k, kb, D), (v, vb, per * D), (q, qb, D))

    def small_copy(i, s):
        return pltpu.make_async_remote_copy(
            src_ref=small[i][0],
            dst_ref=small[i][1].at[me],
            send_sem=fs.at[i, s],
            recv_sem=fr.at[i, s],
            device_id={"head": lax.rem(me + s, n)},
            device_id_type=MESH,
        )

    def small_local(i):
        return pltpu.make_async_copy(small[i][0], small[i][1].at[me], fl.at[i])

    def piece(i, a, dest):
        w = large[i][2]
        return large[i][0].at[:, pl.ds(pl.multiple_of((dest * kheads + a) * w, w), w)]

    def large_copy(i, a, s):
        dest = lax.rem(me + s, n)
        return pltpu.make_async_remote_copy(
            src_ref=piece(i, a, dest),
            dst_ref=large[i][1].at[a, mine, :],
            send_sem=es.at[i, a, s],
            recv_sem=er.at[i, a, s],
            device_id={"head": dest},
            device_id_type=MESH,
        )

    def large_local(i, a):
        return pltpu.make_async_copy(piece(i, a, me), large[i][1].at[a, mine, :], el.at[i, a])

    for i in range(2):
        for s in range(1, n):
            small_copy(i, s).start()
        small_local(i).start()

    def begin(a, carry):
        for i in range(3):
            for s in range(1, n):
                large_copy(i, a, s).start()
            large_local(i, a).start()
        return carry

    lax.fori_loop(0, kheads, begin, 0)
    gate_copy = pltpu.make_async_copy(gate_hbm, gate, gs)
    gate_copy.start()

    ii = lax.broadcasted_iota(jnp.int32, (B, B), 0)
    jj = lax.broadcasted_iota(jnp.int32, (B, B), 1)
    eye = ii == jj
    causal = ii >= jj
    strict = ii > jj
    low = causal.astype(BF)
    upp = (ii <= jj).astype(BF)
    after = (ii < jj).astype(BF)
    ones = jnp.ones((B, B), BF)
    start = jnp.concatenate([jnp.zeros((B, D), F32), eye.astype(F32)], 1)
    for i in range(2):
        for s in range(1, n):
            small_copy(i, s).wait_recv()
        small_local(i).wait()

    def compute(a):
        for i in range(3):
            for s in range(1, n):
                large_copy(i, a, s).wait_recv()
            large_local(i, a).wait()
        first = (me * kheads + a) * per
        sel_t = (
            lax.broadcasted_iota(jnp.int32, (8, wide), 1)
            == lax.broadcasted_iota(jnp.int32, (8, wide), 0) + first
        ).astype(BF)
        lows, reads, rights, info = [], [], [], []
        for b in range(blocks):
            rows = slice(b * B, (b + 1) * B)
            here = slice((b * B) % t, (b * B) % t + B)
            drow = dot(sel_t, deb[b * B // t, :, here]).astype(BF)
            berow = dot(sel_t, beb[b * B // t, :, here])
            bcol = dot_t(low, drow)
            brow = dot(drow, upp)
            becol = dot_t(eye.astype(BF), berow.astype(BF))
            gcol = jnp.exp(bcol)
            grow = jnp.exp(brow)
            ecol = jnp.exp(dot_t(after, drow))
            lastcol = jnp.exp(dot_t(ones, drow))
            kk = kb[a, rows, :]
            qq = qb[a, rows, :]
            g = dot_t(kk, kk)
            diag = jnp.where(eye, g, 0.0)
            rc = lax.rsqrt(jnp.sum(diag, axis=1, keepdims=True) + 1e-6)
            rr = lax.rsqrt(jnp.sum(diag, axis=0, keepdims=True) + 1e-6)
            qf = qq.astype(F32)
            qc = lax.rsqrt(jnp.sum(qf * qf, axis=1, keepdims=True) + 1e-6)
            gn = g * rc * rr
            hn = dot_t(qq, kk) * qc * rr
            kt = jnp.transpose(kk)
            for u in range(per):
                gap = bcol[:, u : u + 1] - brow[u : u + 1, :]
                wts = jnp.where(causal, jnp.exp(jnp.minimum(gap, 0.0)), 0.0)
                lows.append(jnp.where(strict, becol[:, u : u + 1] * wts * gn, 0.0))
                reads.append((wts * hn).astype(BF))
                br = berow[u : u + 1, :]
                rights.append((br, br * grow[u : u + 1, :] * rr))
                info.append((kk, kt, qq, lastcol[:, u : u + 1], ecol[:, u : u + 1] * rc, gcol[:, u : u + 1] * qc))
        inv = unit_lower_inverse(lows, ii, jj)
        fresh, ws = [], []
        for b in range(blocks):
            for u in range(per):
                e = b * per + u
                fresh.append(dot_fe(inv[e] * rights[e][0], vb[a, b * B : (b + 1) * B, u * D : (u + 1) * D]))
                ws.append(dot_fe(inv[e] * rights[e][1], info[e][0]))
        xs = [start for u in range(per)]
        for b in range(blocks):
            rows = slice(b * B, (b + 1) * B)
            for u in range(per):
                e = b * per + u
                kk, kt, qq, last, end, read = info[e]
                d = jnp.concatenate([fresh[e], jnp.zeros((B, D), F32)], 1) - dot_ff(ws[e], xs[u])
                o = dot_ef(reads[e], d) + read * dot_ef(qq, xs[u])
                xs[u] = last * xs[u] + dot_ef(kt, end * d)
                base[a * per + u, rows, :] = o[:, :D]
                r[a * per + u, rows, :] = o[:, D:]
        for u in range(per):
            xf[a * per + u] = xs[u]

    def chain(h):
        return pltpu.make_async_remote_copy(
            src_ref=sout.at[h],
            dst_ref=sin.at[h],
            send_sem=cs.at[h],
            recv_sem=cr.at[h],
            device_id={"ctx": lax.rem(c + 1, m)},
            device_id_type=MESH,
        )

    def send(h, s):
        dest = lax.rem(me + s, n)
        return pltpu.make_async_remote_copy(
            src_ref=core.at[h, pl.ds(pl.multiple_of(dest * t, t), t), :],
            dst_ref=got.at[me * heads + h],
            send_sem=ss.at[h, s],
            recv_sem=rs.at[h, s],
            device_id={"head": dest},
            device_id_type=MESH,
        )

    def carry_on(a):
        for u in range(per):
            h = a * per + u

            @pl.when(c > 0)
            def _():
                chain(h).wait_recv()

            @pl.when(c == 0)
            def _():
                sin[h] = jnp.zeros((D, D), F32)

            @pl.when(c < m - 1)
            def _():
                sout[h] = dot_ff(xf[h, :, D:], sin[h]) + xf[h, :, :D]
                chain(h).start()

        for u in range(per):
            h = a * per + u
            core[h] = (base[h] + dot_ff(r[h], sin[h])).astype(BF)
            for s in range(1, n):
                send(h, s).start()
            got[me * heads + h] = core[h, mine, :]

    scale = gain[...]

    def norm(i):
        x = got[i].astype(F32)
        cols = pl.ds(pl.multiple_of(i * D, D), D)
        g = gate[:, cols].astype(F32)
        y = x * lax.rsqrt(jnp.mean(x * x, axis=-1, keepdims=True) + 1e-6)
        out[:, cols] = (y * scale * (g / (1.0 + jnp.exp(-g)))).astype(BF)

    def close(a):
        for u in range(per):
            h = a * per + u
            norm(me * heads + h)
            for s in range(1, n):
                send(h, s).wait_recv()
                norm(lax.rem(me + n - s, n) * heads + h)

    lag = jnp.minimum(c // 3, kheads - 1)

    def step(j, carry):
        @pl.when(j < kheads)
        def _():
            compute(j)

        now = j - lag

        @pl.when((now >= 0) & (now < kheads))
        def _():
            carry_on(now)

        @pl.when(now == 0)
        def _():
            gate_copy.wait()

        @pl.when((now >= 1) & (now <= kheads))
        def _():
            close(now - 1)

        return carry

    lax.fori_loop(0, 2 * kheads, step, 0)

    def drain(a, carry):
        for i in range(3):
            for s in range(1, n):
                large_copy(i, a, s).wait_send()
        for u in range(per):
            h = a * per + u
            for s in range(1, n):
                send(h, s).wait_send()

            @pl.when(c < m - 1)
            def _():
                chain(h).wait_send()

        return carry

    lax.fori_loop(0, kheads, drain, 0)
    for i in range(2):
        for s in range(1, n):
            small_copy(i, s).wait_send()


def solution(mesh):
    n, m = mesh.shape["head"], mesh.shape["ctx"]

    def local(q, k, v, gate, be, de, gain):
        t, width = v.shape
        heads = width // D // n
        kheads = k.shape[1] // D // n
        per = heads // kheads
        vm = pl.BlockSpec(memory_space=pltpu.VMEM)
        hbm = pl.BlockSpec(memory_space=pl.ANY)
        dma = pltpu.SemaphoreType.DMA
        return pl.pallas_call(
            functools.partial(fused_kernel, n, m, kheads, per),
            out_shape=jax.ShapeDtypeStruct((t, width), BF),
            in_specs=[hbm] * 6 + [vm],
            out_specs=vm,
            scratch_shapes=[
                pltpu.VMEM((kheads, t * n, D), BF),
                pltpu.VMEM((kheads, t * n, D), BF),
                pltpu.VMEM((kheads, t * n, per * D), BF),
                pltpu.VMEM((n, be.shape[1], t), BF),
                pltpu.VMEM((n, de.shape[1], t), BF),
                pltpu.VMEM((t, width), BF),
                pltpu.VMEM((heads, D, 2 * D), F32),
                pltpu.VMEM((heads, t * n, D), F32),
                pltpu.VMEM((heads, t * n, D), F32),
                pltpu.VMEM((heads, D, D), F32),
                pltpu.VMEM((heads, D, D), F32),
                pltpu.VMEM((heads, t * n, D), BF),
                pltpu.VMEM((heads * n, t, D), BF),
                dma((3, kheads, n)),
                dma((3, kheads, n)),
                dma((3, kheads)),
                dma((2, n)),
                dma((2, n)),
                dma((2,)),
                dma,
                dma((heads,)),
                dma((heads,)),
                dma((heads, n)),
                dma((heads, n)),
            ],
            compiler_params=pltpu.CompilerParams(
                collective_id=0, has_side_effects=True, vmem_limit_bytes=56 << 20
            ),
        )(q, k, v, be.T, de.T, gate, gain.reshape(1, D))

    rows = P(("ctx", "head"), None)
    return jax.shard_map(
        local, mesh=mesh, in_specs=(rows,) * 6 + (P(),), out_specs=rows, check_vma=False
    )
```

```python
import functools

import jax
import jax.numpy as jnp
from jax import lax
from jax.experimental import pallas as pl
from jax.experimental.pallas import tpu as pltpu
from jax.sharding import PartitionSpec as P

D = 128
B = 128
F32 = jnp.float32
BF = jnp.bfloat16
MESH = pl.DeviceIdType.MESH


def split(x):
    hi = x.astype(BF)
    return hi, (x - hi.astype(F32)).astype(BF)


def dot(a, b):
    return jnp.dot(a, b, preferred_element_type=F32)


def dot_t(a, b):
    return lax.dot_general(a, b, (((1,), (1,)), ((), ())), preferred_element_type=F32)


def dot_b(a, b):
    return dot(a.astype(BF), b.astype(BF))


def dot_fe(a, b):
    hi, lo = split(a)
    return dot(jnp.concatenate([hi, lo], 1), jnp.concatenate([b, b], 0))


def dot_ef(a, b):
    hi, lo = split(b)
    return dot(jnp.concatenate([a, a], 1), jnp.concatenate([hi, lo], 0))


def dot_ff(a, b):
    ah, al = split(a)
    bh, bl = split(b)
    return dot(jnp.concatenate([ah, ah], 1), jnp.concatenate([bh, bl], 0)) + dot(al, bh)


def unit_lower_inverse(lows, ii, jj):
    eye = (ii == jj).astype(F32)

    def same(w):
        return (ii // w) == (jj // w)

    base = same(16)
    p = [jnp.where(base, -x, 0.0) for x in lows]
    t = [eye + x for x in p]
    for _ in range(3):
        pb = [x.astype(BF) for x in p]
        p = [dot(x, x) for x in pb]
        t = [y + dot_b(y, x) for y, x in zip(t, p)]
    w = 16
    while w < B:
        off = same(2 * w) & ~same(w)
        tb = [y.astype(BF) for y in t]
        z = [dot(jnp.where(off, x, 0.0).astype(BF), y) for x, y in zip(lows, tb)]
        t = [y - dot(yb, x.astype(BF)) for y, yb, x in zip(t, tb, z)]
        w *= 2
    return t


def fused_kernel(
    n, m, kheads, per,
    q, k, v, be, de, gate_hbm, gain,
    out,
    qb, kb, vb, beb, deb, gate, xf, base, r, sin, sout, core, got,
    es, er, el, fs, fr, fl, gs, cs, cr, ss, rs,
):
    me = lax.axis_index("head")
    c = lax.axis_index("ctx")
    heads = kheads * per
    t = q.shape[0]
    wide = be.shape[0]
    blocks = t * n // B
    barrier = pltpu.get_barrier_semaphore()
    for s in range(1, n):
        pl.semaphore_signal(barrier, inc=1, device_id={"head": lax.rem(me + s, n)}, device_id_type=MESH)
    for s in (1, m - 1):
        pl.semaphore_signal(barrier, inc=1, device_id={"ctx": lax.rem(c + s, m)}, device_id_type=MESH)
    pl.semaphore_wait(barrier, n + 1)

    mine = pl.ds(pl.multiple_of(me * t, t), t)
    small = ((de, deb), (be, beb))
    large = ((k, kb, D), (v, vb, per * D), (q, qb, D))

    def small_copy(i, s):
        return pltpu.make_async_remote_copy(
            src_ref=small[i][0],
            dst_ref=small[i][1].at[me],
            send_sem=fs.at[i, s],
            recv_sem=fr.at[i, s],
            device_id={"head": lax.rem(me + s, n)},
            device_id_type=MESH,
        )

    def small_local(i):
        return pltpu.make_async_copy(small[i][0], small[i][1].at[me], fl.at[i])

    def piece(i, a, dest):
        w = large[i][2]
        return large[i][0].at[:, pl.ds(pl.multiple_of((dest * kheads + a) * w, w), w)]

    def large_copy(i, a, s):
        dest = lax.rem(me + s, n)
        return pltpu.make_async_remote_copy(
            src_ref=piece(i, a, dest),
            dst_ref=large[i][1].at[a, mine, :],
            send_sem=es.at[i, a, s],
            recv_sem=er.at[i, a, s],
            device_id={"head": dest},
            device_id_type=MESH,
        )

    def large_local(i, a):
        return pltpu.make_async_copy(piece(i, a, me), large[i][1].at[a, mine, :], el.at[i, a])

    for i in range(2):
        for s in range(1, n):
            small_copy(i, s).start()
        small_local(i).start()

    def begin(a, carry):
        for i in range(3):
            for s in range(1, n):
                large_copy(i, a, s).start()
            large_local(i, a).start()
        return carry

    lax.fori_loop(0, kheads, begin, 0)
    gate_copy = pltpu.make_async_copy(gate_hbm, gate, gs)
    gate_copy.start()

    ii = lax.broadcasted_iota(jnp.int32, (B, B), 0)
    jj = lax.broadcasted_iota(jnp.int32, (B, B), 1)
    eye = ii == jj
    causal = ii >= jj
    strict = ii > jj
    low = causal.astype(BF)
    upp = (ii <= jj).astype(BF)
    after = (ii < jj).astype(BF)
    ones = jnp.ones((B, B), BF)
    for i in range(2):
        for s in range(1, n):
            small_copy(i, s).wait_recv()
        small_local(i).wait()

    def compute(a):
        for i in range(3):
            for s in range(1, n):
                large_copy(i, a, s).wait_recv()
            large_local(i, a).wait()
        first = (me * kheads + a) * per
        sel_t = (
            lax.broadcasted_iota(jnp.int32, (8, wide), 1)
            == lax.broadcasted_iota(jnp.int32, (8, wide), 0) + first
        ).astype(BF)
        lows, reads, rights, info = [], [], [], []
        for b in range(blocks):
            rows = slice(b * B, (b + 1) * B)
            here = slice((b * B) % t, (b * B) % t + B)
            drow = dot(sel_t, deb[b * B // t, :, here]).astype(BF)
            berow = dot(sel_t, beb[b * B // t, :, here])
            bcol = dot_t(low, drow)
            brow = dot(drow, upp)
            becol = dot_t(eye.astype(BF), berow.astype(BF))
            gcol = jnp.exp(bcol)
            grow = jnp.exp(brow)
            ecol = jnp.exp(dot_t(after, drow))
            lastcol = jnp.exp(dot_t(ones, drow))
            kk = kb[a, rows, :]
            qq = qb[a, rows, :]
            g = dot_t(kk, kk)
            diag = jnp.where(eye, g, 0.0)
            rc = lax.rsqrt(jnp.sum(diag, axis=1, keepdims=True) + 1e-6)
            rr = lax.rsqrt(jnp.sum(diag, axis=0, keepdims=True) + 1e-6)
            qf = qq.astype(F32)
            qc = lax.rsqrt(jnp.sum(qf * qf, axis=1, keepdims=True) + 1e-6)
            gn = g * rc * rr
            hn = dot_t(qq, kk) * qc * rr
            kt = jnp.transpose(kk)
            for u in range(per):
                gap = bcol[:, u : u + 1] - brow[u : u + 1, :]
                wts = jnp.where(causal, jnp.exp(jnp.minimum(gap, 0.0)), 0.0)
                lows.append(jnp.where(strict, becol[:, u : u + 1] * wts * gn, 0.0))
                reads.append((wts * hn).astype(BF))
                br = berow[u : u + 1, :]
                rights.append((br, br * grow[u : u + 1, :] * rr))
                info.append((kk, kt, qq, lastcol[:, u : u + 1], ecol[:, u : u + 1] * rc, gcol[:, u : u + 1] * qc))
        inv = unit_lower_inverse(lows, ii, jj)
        zero = jnp.zeros((B, D), F32)
        uws = []
        for b in range(blocks):
            for u in range(per):
                e = b * per + u
                vv = vb[a, b * B : (b + 1) * B, u * D : (u + 1) * D]
                uws.append(
                    jnp.concatenate(
                        [dot_fe(inv[e] * rights[e][0], vv), dot_fe(inv[e] * rights[e][1], info[e][0])], 1
                    )
                )
        steps = []
        for e, uw in enumerate(uws):
            kk, kt, qq, last, end, read = info[e]
            tw = dot_ef(kt, end * uw)
            steps.append((tw[:, :D], jnp.where(eye, last, 0.0) - tw[:, D:]))
        xs = [[jnp.concatenate(steps[u], 1)] for u in range(per)]
        for b in range(1, blocks):
            for u in range(per):
                written, trans = steps[b * per + u]
                xs[u].append(dot_ff(trans, xs[u][-1]) + jnp.concatenate([written, zero], 1))
        for u in range(per):
            xf[a * per + u] = xs[u][-1]
        for b in range(blocks):
            rows = slice(b * B, (b + 1) * B)
            for u in range(per):
                e = b * per + u
                kk, kt, qq, last, end, read = info[e]
                lr = dot_ef(reads[e], uws[e])
                near = lr[:, :D]
                far = read * qq.astype(F32) - lr[:, D:]
                if b > 0:
                    o = dot_ef(far.astype(BF), xs[u][b - 1])
                    near = near + o[:, :D]
                    far = o[:, D:]
                base[a * per + u, rows, :] = near
                r[a * per + u, rows, :] = far.astype(BF)

    def chain(h):
        return pltpu.make_async_remote_copy(
            src_ref=sout.at[h],
            dst_ref=sin.at[h],
            send_sem=cs.at[h],
            recv_sem=cr.at[h],
            device_id={"ctx": lax.rem(c + 1, m)},
            device_id_type=MESH,
        )

    def send(h, s):
        dest = lax.rem(me + s, n)
        return pltpu.make_async_remote_copy(
            src_ref=core.at[h, pl.ds(pl.multiple_of(dest * t, t), t), :],
            dst_ref=got.at[me * heads + h],
            send_sem=ss.at[h, s],
            recv_sem=rs.at[h, s],
            device_id={"head": dest},
            device_id_type=MESH,
        )

    def carry_on(a):
        for u in range(per):
            h = a * per + u

            @pl.when(c > 0)
            def _():
                chain(h).wait_recv()

            @pl.when(c == 0)
            def _():
                sin[h] = jnp.zeros((D, D), F32)

            @pl.when(c < m - 1)
            def _():
                sout[h] = dot_ff(xf[h, :, D:], sin[h]) + xf[h, :, :D]
                chain(h).start()

        for u in range(per):
            h = a * per + u
            core[h] = (base[h] + dot_ef(r[h], sin[h])).astype(BF)
            for s in range(1, n):
                send(h, s).start()
            got[me * heads + h] = core[h, mine, :]

    scale = gain[...]

    def norm(i):
        x = got[i].astype(F32)
        cols = pl.ds(pl.multiple_of(i * D, D), D)
        g = gate[:, cols].astype(F32)
        y = x * lax.rsqrt(jnp.mean(x * x, axis=-1, keepdims=True) + 1e-6)
        out[:, cols] = (y * scale * (g / (1.0 + jnp.exp(-g)))).astype(BF)

    def close(a):
        for u in range(per):
            h = a * per + u
            norm(me * heads + h)
            for s in range(1, n):
                send(h, s).wait_recv()
                norm(lax.rem(me + n - s, n) * heads + h)

    lag = jnp.minimum(c // 3, kheads - 1)

    def step(j, carry):
        @pl.when(j < kheads)
        def _():
            compute(j)

        now = j - lag

        @pl.when((now >= 0) & (now < kheads))
        def _():
            carry_on(now)

        @pl.when(now == 0)
        def _():
            gate_copy.wait()

        @pl.when((now >= 1) & (now <= kheads))
        def _():
            close(now - 1)

        return carry

    lax.fori_loop(0, 2 * kheads, step, 0)

    def drain(a, carry):
        for i in range(3):
            for s in range(1, n):
                large_copy(i, a, s).wait_send()
        for u in range(per):
            h = a * per + u
            for s in range(1, n):
                send(h, s).wait_send()

            @pl.when(c < m - 1)
            def _():
                chain(h).wait_send()

        return carry

    lax.fori_loop(0, kheads, drain, 0)
    for i in range(2):
        for s in range(1, n):
            small_copy(i, s).wait_send()


def solution(mesh):
    n, m = mesh.shape["head"], mesh.shape["ctx"]

    def local(q, k, v, gate, be, de, gain):
        t, width = v.shape
        heads = width // D // n
        kheads = k.shape[1] // D // n
        per = heads // kheads
        vm = pl.BlockSpec(memory_space=pltpu.VMEM)
        hbm = pl.BlockSpec(memory_space=pl.ANY)
        dma = pltpu.SemaphoreType.DMA
        return pl.pallas_call(
            functools.partial(fused_kernel, n, m, kheads, per),
            out_shape=jax.ShapeDtypeStruct((t, width), BF),
            in_specs=[hbm] * 6 + [vm],
            out_specs=vm,
            scratch_shapes=[
                pltpu.VMEM((kheads, t * n, D), BF),
                pltpu.VMEM((kheads, t * n, D), BF),
                pltpu.VMEM((kheads, t * n, per * D), BF),
                pltpu.VMEM((n, be.shape[1], t), BF),
                pltpu.VMEM((n, de.shape[1], t), BF),
                pltpu.VMEM((t, width), BF),
                pltpu.VMEM((heads, D, 2 * D), F32),
                pltpu.VMEM((heads, t * n, D), F32),
                pltpu.VMEM((heads, t * n, D), BF),
                pltpu.VMEM((heads, D, D), F32),
                pltpu.VMEM((heads, D, D), F32),
                pltpu.VMEM((heads, t * n, D), BF),
                pltpu.VMEM((heads * n, t, D), BF),
                dma((3, kheads, n)),
                dma((3, kheads, n)),
                dma((3, kheads)),
                dma((2, n)),
                dma((2, n)),
                dma((2,)),
                dma,
                dma((heads,)),
                dma((heads,)),
                dma((heads, n)),
                dma((heads, n)),
            ],
            compiler_params=pltpu.CompilerParams(
                collective_id=0, has_side_effects=True, vmem_limit_bytes=56 << 20
            ),
        )(q, k, v, be.T, de.T, gate, gain.reshape(1, D))

    rows = P(("ctx", "head"), None)
    return jax.shard_map(
        local, mesh=mesh, in_specs=(rows,) * 6 + (P(),), out_specs=rows, check_vma=False
    )
```
